32 devices in a mesh: phonon: 2 (over y), row: 4 (over x, core), beam: 4 (over z).
Axes of the slice: x: 2, y: 2, z: 4, core: 2. Of those that a mesh axis runs over, the one named last changes fastest.
Arguments:
- spectra: float32 [2, 8, 512, 512], P(None, ('phonon', 'beam'), 'row'), parts along dimension 1, may hold values from -6 to 6
- potential: float32 [1024, 512], P(('phonon', 'beam'), 'row'), parts along dimension 0, may hold values from -3.140625 to 3.140625
- amp_re: float32 [4], replicated, may hold values from -0.75 to 0.75
- amp_im: float32 [4], replicated, may hold values from -0.75 to 0.75
- beam_freq: int32 [4, 2], replicated, may hold values from -32 to 31
- probe_corners: int32 [16, 2], replicated, may hold values from 0 to 511, as said below
- slot_table: int32 [4, 4, 2], replicated, may hold values from 0 to 16, as said below
Outputs:
- patterns: float32 [8, 4, 2, 128, 128], P(('phonon', 'beam'), 'row'), parts along dimension 0
The draws below stay inside these ranges and needn't reach their ends.
There are 2 independent parts, one for each index of `phonon`. The reference program is written for one: setup_inputs(seed, part) draws one part's arguments, and reference() takes and returns one part's arrays. A program takes and returns all parts, laid end to end along the dimension named above; an argument that names none is the same for every part. Nothing has to cross between parts.
Inputs may be any that keep to these rules, and one draw needn't show every extreme that they name: `probe_corners`: the corner of each probe lies in the tile (corner row // 128, corner column // 128) whose list in slot_table names that probe. slot_table[i, j] lists in rising order the probes whose window corner lies in tile rows i * 128 to (i + 1) * 128 - 1 and columns j * 128 to (j + 1) * 128 - 1, then the value 16 in every unused slot; each probe is listed exactly once; in every draw some tile lists 2 probes.
All inputs are finite; a program needn't handle non-finite values.
Results may differ from the reference program's by a relative error of at most 0.0003.
Values sent between devices are 32-bit elements; how exact they have to be, the bound alone decides.
No kernel may reach another device: no remote copies, remote signals or barrier semaphores. Data moves between devices by JAX's collectives and lax.ppermute only.
A program may use at most 64 MiB of HBM per device.

```python
import math
import jax
import jax.numpy as jnp
from jax import lax

GRID = 512
WIN = 128
SLOTS = 2
BEAMS = 4
TILES = 16
PROBES = 16
TILE_ROWS = 128
TILE_COLS = 128
N_ROW = 4
N_BEAM = 4


def probe_plan(key):
    keys = jax.random.split(jax.random.fold_in(key, 7), 5)
    slots_all = jax.random.permutation(keys[0], TILES * SLOTS).astype(jnp.int32)
    tile_all = slots_all // SLOTS
    crowded = jax.random.randint(keys[1], (), 0, TILES).astype(jnp.int32)
    order = jnp.argsort((tile_all == crowded).astype(jnp.int32), stable=True)
    remaining = tile_all[order][:PROBES - SLOTS]
    tile_seq = jnp.concatenate([jnp.full((SLOTS,), crowded, jnp.int32), remaining.astype(jnp.int32)])
    shuffle = jax.random.permutation(keys[2], PROBES)
    tile_of = tile_seq[shuffle]
    row_inside = jax.random.randint(keys[3], (PROBES,), 0, TILE_ROWS).astype(jnp.int32)
    col_inside = jax.random.randint(keys[4], (PROBES,), 0, TILE_COLS).astype(jnp.int32)
    corner_y = tile_of // N_ROW * TILE_ROWS + row_inside
    corner_x = tile_of % N_ROW * TILE_COLS + col_inside
    corners = jnp.stack([corner_y, corner_x], axis=1).astype(jnp.int32)
    sorted_ids = jnp.argsort(tile_of, stable=True).astype(jnp.int32)
    tile_sorted = tile_of[sorted_ids]
    first_pos = jnp.searchsorted(tile_sorted, jnp.arange(TILES, dtype=jnp.int32)).astype(jnp.int32)
    rank_in = jnp.arange(PROBES, dtype=jnp.int32) - first_pos[tile_sorted]
    table = jnp.full((TILES * SLOTS,), PROBES, jnp.int32).at[tile_sorted * SLOTS + rank_in].set(sorted_ids)
    return (corners, table.reshape(N_BEAM, N_ROW, SLOTS))


def draw_probe_corners(key, part):
    return probe_plan(key)[0]


def draw_slot_table(key, part):
    return probe_plan(key)[1]


def touch_ends(values, key, least, largest):
    spot = [jax.random.randint(jax.random.fold_in(key, axis), (), 0, length) for axis, length in enumerate(values.shape)]
    longest = values.shape.index(max(values.shape))
    neighbour = spot[:longest] + [(spot[longest] + 1) % values.shape[longest]] + spot[longest + 1:]
    return values.at[tuple(spot)].set(least).at[tuple(neighbour)].set(largest)


def steps_of(key, shape, pieces, smallest, high):
    factor_of, own = 1.0, jax.random.fold_in(key, 6)
    for axis_at, blocks in pieces:
        steps = jnp.exp(jax.random.uniform(jax.random.fold_in(own, axis_at), (blocks,), jnp.float32, smallest / len(pieces), high / len(pieces)))
        factor_of = factor_of * jnp.repeat(steps, shape[axis_at] // blocks).reshape([-1 if axis == axis_at else 1 for axis in range(len(shape))])
    return factor_of


def gaussian(key, extent, scale, reach, cuts=(), kind=jnp.bfloat16):
    factor_of = steps_of(key, extent, cuts, -0.22, 0.18) if cuts else 1.0
    drawn = jax.random.normal(key, extent, jnp.float32) * scale * factor_of
    return jnp.minimum(jnp.maximum(drawn, -reach), reach).astype(kind)


def setup_inputs(seed: int = 0, part: int = 0) -> dict:
    arg_keys = jax.random.split(jax.random.key(seed), 8)
    part_keys = jax.random.split(jax.random.fold_in(arg_keys[7], part), 8)
    spectra = gaussian(part_keys[0], (2, BEAMS, GRID, GRID), 1.0, 6.0, ((1, 4), (2, 4)), jnp.float32)
    potential = jnp.clip(jax.random.uniform(part_keys[1], (GRID, GRID), jnp.float32, -3.140625, 3.140625), -3.140625, 3.140625)
    amp_re = gaussian(arg_keys[2], (BEAMS,), 0.125, 0.75, (), jnp.float32)
    amp_im = gaussian(arg_keys[3], (BEAMS,), 0.125, 0.75, (), jnp.float32)
    beam_freq = touch_ends(jax.random.randint(arg_keys[4], (BEAMS, 2), 0 - GRID // 16, GRID // 16), jax.random.fold_in(arg_keys[4], 1), 0 - GRID // 16, (GRID // 16) - 1).astype(jnp.int32)
    probe_corners = draw_probe_corners(jax.random.fold_in(arg_keys[7], 71), part)
    slot_table = draw_slot_table(jax.random.fold_in(arg_keys[7], 71), part)
    return {"spectra": spectra, "potential": potential, "amp_re": amp_re, "amp_im": amp_im, "beam_freq": beam_freq, "probe_corners": probe_corners, "slot_table": slot_table}


prop_coef = 3e-5
highest = lax.Precision.HIGHEST


def signed_freq(index, length):
    return jnp.where(index < length // 2, index, index - length)


def probe_coeffs(slot_ids, corners, amp_re, amp_im, beam_freq, grid_len):
    total = corners.shape[0]
    slot_live = (slot_ids < total).astype(jnp.float32)[..., None]
    safe_ids = jnp.minimum(slot_ids, total - 1)
    corner_y = corners[safe_ids, 0][..., None]
    corner_x = corners[safe_ids, 1][..., None]
    turns = jnp.mod(corner_y * beam_freq[:, 0] + corner_x * beam_freq[:, 1], grid_len)
    angle = (-2.0 * math.pi / grid_len) * turns.astype(jnp.float32)
    cosine = jnp.cos(angle)
    sine_val = jnp.sin(angle)
    return (amp_re * cosine - amp_im * sine_val) * slot_live, (amp_re * sine_val + amp_im * cosine) * slot_live


def reference(spectra, potential, amp_re, amp_im, beam_freq, probe_corners, slot_table):
    freq_all = signed_freq(jnp.arange(GRID, dtype=jnp.int32), GRID)
    squared = freq_all[:, None] * freq_all[:, None] + freq_all[None, :] * freq_all[None, :]
    prop_phase = -prop_coef * squared.astype(jnp.float32)
    propagator = lax.complex(jnp.cos(prop_phase), jnp.sin(prop_phase))
    shifted = lax.complex(spectra[0], spectra[1]) * propagator
    transmit = lax.complex(jnp.cos(potential), jnp.sin(potential))
    exit_wave = jnp.fft.ifft2(shifted, norm="ortho") * transmit
    offsets = jnp.arange(WIN, dtype=jnp.int32)

    def one_probe(probe_id):
        rows_idx = jnp.mod(probe_corners[probe_id, 0] + offsets, GRID)
        cols_idx = jnp.mod(probe_corners[probe_id, 1] + offsets, GRID)
        patch = jnp.take(jnp.take(exit_wave, rows_idx, axis=1), cols_idx, axis=2)
        coef_re, coef_im = probe_coeffs(probe_id, probe_corners, amp_re, amp_im, beam_freq, GRID)
        weights = lax.complex(coef_re, coef_im)
        window = jnp.einsum("b,buv->uv", weights, patch, precision=highest)
        diffracted = jnp.fft.fft2(window, norm="ortho")
        return jnp.real(diffracted) * jnp.real(diffracted) + jnp.imag(diffracted) * jnp.imag(diffracted)

    intensity = lax.map(one_probe, jnp.arange(PROBES, dtype=jnp.int32))
    safe_ids = jnp.minimum(slot_table, PROBES - 1)
    slot_live = (slot_table < PROBES).astype(jnp.float32)
    return intensity[safe_ids] * slot_live[..., None, None]
```

```python
import functools
import math

import jax
import jax.numpy as jnp
import numpy as np
from jax import lax
from jax.experimental import pallas as pl
from jax.experimental.pallas import tpu as pltpu
from jax.sharding import PartitionSpec as P

WIN = 128

prop_coef = 3e-05
f32, bf16 = jnp.float32, jnp.bfloat16


def shift(shard, axis, by):
    devices = lax.axis_size(axis)
    return lax.ppermute(shard, axis, [(i, (i + by) % devices) for i in range(devices)])


def split_table(table):
    high = np.asarray(table, np.float32).astype(bf16)
    low = (np.asarray(table, np.float64) - high.astype(np.float64)).astype(np.float32).astype(bf16)
    return high, low


def wave_table(length):
    index = np.arange(length)
    freq = np.where(index < length // 2, index, index - length).astype(np.float64)
    turns = (index[:, None] * index[None, :]) % length
    angle = 2.0 * math.pi / length * turns - prop_coef * (freq * freq)[:, None]
    return np.cos(angle) / math.sqrt(length), np.sin(angle) / math.sqrt(length)


def row_tables(length, tile_cols, tiles):
    real, imag = wave_table(length)
    cols = (np.arange(tiles)[:, None] * tile_cols + np.arange(WIN)[None, :]) % length
    both = np.concatenate([real[:, cols], imag[:, cols]], axis=2)
    return split_table(np.moveaxis(both, 1, 0))


def column_tables(length):
    radix = length // WIN
    real, imag = wave_table(length)
    parts = []
    for k0 in range(radix):
        both = np.concatenate([real[k0::radix, :WIN].T, imag[k0::radix, :WIN].T], axis=0)
        high, low = split_table(both)
        parts.append(np.concatenate([high, low, high], axis=1))
    return np.stack(parts)


def window_tables():
    index = np.arange(WIN)
    angle = -2.0 * math.pi / WIN * ((index[:, None] * index[None, :]) % WIN)
    real, imag = np.cos(angle) / math.sqrt(WIN), np.sin(angle) / math.sqrt(WIN)
    left = np.concatenate([np.concatenate([real, -imag], 1), np.concatenate([imag, real], 1)], 0)
    right = np.concatenate([np.concatenate([real, imag], 1), np.concatenate([-imag, real], 1)], 0)
    return split_table(left) + split_table(right)


def split(value):
    high = value.astype(bf16)
    return high, (value - high.astype(f32)).astype(bf16)


def mul(left, right):
    return jnp.dot(left, right, preferred_element_type=f32)


def row_kernel(tiles, step, spectra, high, low, *messages):
    me = lax.axis_index("row")
    rows = spectra.shape[2]
    lhs = jnp.concatenate([spectra[0, 0], spectra[1, 0]], axis=0)
    lhs_high, lhs_low = split(lhs)
    for k in range(tiles):
        tile = lax.rem(me + k, tiles)
        table = high[tile]
        both = mul(lhs_high, table) + mul(lhs_low, table) + mul(lhs_high, low[tile])
        real = both[:rows, :WIN] - both[rows:, WIN:]
        imag = both[:rows, WIN:] + both[rows:, :WIN]
        for block, to in enumerate((k, (k - step) % tiles)):
            messages[to][block, 0] = real
            messages[to][block, 1] = imag


def prep_kernel(sizes, slots_ref, corners, freq, amp_re, amp_im, cosine, sine, params):
    row_tiles, col_tiles, slots, probes, tile_rows, tile_cols, grid_len = sizes
    beam_pos, row_pos = lax.axis_index("beam"), lax.axis_index("row")
    for k in range(row_tiles):
        tile = lax.rem(beam_pos + k, row_tiles)
        for s in range(slots):
            probe = slots_ref[(tile * col_tiles + row_pos) * slots + s]
            live = (probe < probes).astype(f32)
            safe = jnp.minimum(probe, probes - 1)
            top, left = corners[2 * safe], corners[2 * safe + 1]
            turns = lax.rem(top * freq[2 * beam_pos] + left * freq[2 * beam_pos + 1], grid_len)
            turns = lax.rem(turns + grid_len, grid_len)
            re, im = amp_re[beam_pos] * live, amp_im[beam_pos] * live
            c, n = cosine[turns], sine[turns]
            values = [
                re * c - im * n,
                re * n + im * c,
                jnp.clip(top - tile * tile_rows, 0, tile_rows - 1).astype(f32),
                jnp.clip(left - row_pos * tile_cols, 0, tile_cols - 1).astype(f32),
            ]
            for at, value in enumerate(values):
                params[k * slots + s, at] = jnp.full((WIN,), value, f32)


def masks_of(params, at):
    row = lax.broadcasted_iota(jnp.int32, (WIN, WIN), 0).astype(f32)
    col = lax.broadcasted_iota(jnp.int32, (WIN, WIN), 1).astype(f32)
    return row >= params[at, 2:3, :], col >= params[at, 3:4, :]


def pick(rows_here, cols_here, near_near, near_far, far_near, far_far):
    return jnp.where(
        rows_here,
        jnp.where(cols_here, near_near, near_far),
        jnp.where(cols_here, far_near, far_far),
    )


def transmit_kernel(slots, phase, params, out):
    for s in range(slots):
        rows_here, cols_here = masks_of(params, s)
        value = pick(
            rows_here,
            cols_here,
            phase[:WIN, :WIN],
            phase[:WIN, WIN:],
            phase[WIN:, :WIN],
            phase[WIN:, WIN:],
        )
        out[s, :, :WIN] = jnp.cos(value)
        out[s, :, WIN:] = jnp.sin(value)


def column_kernel(sizes, *refs):
    sources, radix, row_tiles, slots, tile_rows = sizes
    arrived, (table, params) = refs[:sources], refs[sources : sources + 2]
    sends = refs[sources + 2 : sources + 2 + row_tiles]
    gathered, waves = refs[sources + 2 + row_tiles :]
    row_pos, beam_pos = lax.axis_index("row"), lax.axis_index("beam")
    part = arrived[0].shape[2] // radix
    for k in range(sources):
        source = lax.rem(row_pos + sources - k, sources)
        at = pl.ds(pl.multiple_of(source * part, part), part)
        for k0 in range(radix):
            for block in range(2):
                for c in range(2):
                    cols = slice((2 * block + c) * WIN, (2 * block + c + 1) * WIN)
                    gathered[k0, at, cols] = arrived[k][
                        block, c, pl.ds(k0, part, stride=radix), :
                    ]
    pieces = []
    for k0 in range(radix):
        high, low = split(gathered[k0])
        both = mul(table[k0], jnp.concatenate([high, high, low], axis=0))
        halves = []
        for block in range(2):
            at = block * 2 * WIN
            real = both[:WIN, at : at + WIN] - both[WIN:, at + WIN : at + 2 * WIN]
            imag = both[:WIN, at + WIN : at + 2 * WIN] + both[WIN:, at : at + WIN]
            halves.append((real, imag))
        pieces.append(halves)
    grid_len = radix * WIN
    for block in range(2):
        at = block * 2 * WIN
        for a in range(radix):
            real = imag = None
            for k0 in range(radix):
                re, im = pieces[k0][block]
                quarter = (4 * k0 * a // radix) % 4
                re, im = [(re, im), (-im, re), (-re, -im), (im, -re)][quarter]
                real = re if real is None else real + re
                imag = im if imag is None else imag + im
            waves[a * WIN : (a + 1) * WIN, at : at + WIN] = real
            waves[a * WIN : (a + 1) * WIN, at + WIN : at + 2 * WIN] = imag
            if a == 0:
                waves[grid_len : grid_len + WIN, at : at + WIN] = real
                waves[grid_len : grid_len + WIN, at + WIN : at + 2 * WIN] = imag
    for k in range(row_tiles):
        start = lax.rem(beam_pos + k, row_tiles) * tile_rows
        near = pl.ds(pl.multiple_of(start, 8), WIN)
        far = pl.ds(pl.multiple_of(lax.rem(start + WIN, grid_len), 8), WIN)
        for s in range(slots):
            which = k * slots + s
            rows_here, cols_here = masks_of(params, which)
            picked = []
            for c in range(2):
                first = slice(c * WIN, (c + 1) * WIN)
                second = slice((c + 2) * WIN, (c + 3) * WIN)
                picked.append(
                    pick(
                        rows_here,
                        cols_here,
                        waves[near, first],
                        waves[near, second],
                        waves[far, first],
                        waves[far, second],
                    )
                )
            re, im = picked
            coef_re, coef_im = params[which, 0:1, :], params[which, 1:2, :]
            sends[k][s, :, :WIN] = re * coef_re - im * coef_im
            sends[k][s, :, WIN:] = re * coef_im + im * coef_re


def pattern_kernel(sources, slots, *refs):
    arrived = refs[:sources]
    transmit, left_high, left_low, right_high, right_low, out = refs[sources:]
    tops, bottoms = [], []
    for s in range(slots):
        total = arrived[0][s]
        for k in range(1, sources):
            total = total + arrived[k][s]
        re, im = total[:, :WIN], total[:, WIN:]
        t_re, t_im = transmit[s, :, :WIN], transmit[s, :, WIN:]
        tops.append(re * t_re - im * t_im)
        bottoms.append(re * t_im + im * t_re)
    window = jnp.concatenate(
        [jnp.concatenate(tops, axis=1), jnp.concatenate(bottoms, axis=1)], axis=0
    )
    high, low = split(window)
    inner = mul(left_high[...], high) + mul(left_high[...], low) + mul(left_low[...], high)
    inner = jnp.concatenate(
        [
            jnp.concatenate(
                [inner[:WIN, s * WIN : (s + 1) * WIN], inner[WIN:, s * WIN : (s + 1) * WIN]], axis=1
            )
            for s in range(slots)
        ],
        axis=0,
    )
    high, low = split(inner)
    outer = mul(high, right_high[...]) + mul(low, right_high[...]) + mul(high, right_low[...])
    power = outer[:, :WIN] * outer[:, :WIN] + outer[:, WIN:] * outer[:, WIN:]
    for s in range(slots):
        out[0, 0, s] = power[s * WIN : (s + 1) * WIN]


def call(kernel, name, ins, outs, smem=(), scratch=(), flops=0, moved=0):
    vmem, scalar = pl.BlockSpec(memory_space=pltpu.VMEM), pl.BlockSpec(memory_space=pltpu.SMEM)
    return pl.pallas_call(
        kernel,
        name=name,
        out_shape=outs,
        in_specs=[scalar if at in smem else vmem for at in range(len(ins))],
        out_specs=jax.tree.map(lambda _: vmem, outs),
        scratch_shapes=list(scratch),
        cost_estimate=pl.CostEstimate(flops=flops, bytes_accessed=moved, transcendentals=0),
    )(*ins)


def local(spectra, potential, amp_re, amp_im, beam_freq, probe_corners, slot_table):
    ky_rows, grid_len = spectra.shape[2], spectra.shape[3]
    tile_rows, tile_cols = potential.shape
    row_tiles, col_tiles, slots = slot_table.shape
    probes = probe_corners.shape[0]
    radix = grid_len // WIN

    def floats(*shape):
        return jax.ShapeDtypeStruct(shape, f32)

    row_high, row_low = row_tables(grid_len, tile_cols, col_tiles)
    messages = call(
        functools.partial(row_kernel, col_tiles, WIN // tile_cols),
        "row_transform",
        (spectra, jnp.asarray(row_high), jnp.asarray(row_low)),
        [floats(2, 2, ky_rows, WIN)] * col_tiles,
        flops=24 * ky_rows * grid_len * WIN * col_tiles,
        moved=8 << 20,
    )
    arrived = [messages[0]] + [shift(messages[k], "row", k) for k in range(1, col_tiles)]

    index = np.arange(grid_len)
    angle = -2.0 * math.pi / grid_len * index
    params = call(
        functools.partial(
            prep_kernel,
            (row_tiles, col_tiles, slots, probes, tile_rows, tile_cols, grid_len),
        ),
        "slot_parameters",
        (
            slot_table.reshape(-1),
            probe_corners.reshape(-1),
            beam_freq.reshape(-1),
            amp_re,
            amp_im,
            jnp.asarray(np.cos(angle), f32),
            jnp.asarray(np.sin(angle), f32),
        ),
        floats(row_tiles * slots, 8, WIN),
        smem=range(7),
    )

    below = [potential] + [shift(potential, "beam", -k) for k in range(1, WIN // tile_rows + 1)]
    tall = jnp.concatenate(below, axis=0)
    beside = [tall] + [shift(tall, "row", -k) for k in range(1, WIN // tile_cols + 1)]
    phase = jnp.concatenate(beside, axis=1)
    phase = jnp.pad(phase, [(0, 2 * WIN - length) for length in phase.shape])
    transmit = call(
        functools.partial(transmit_kernel, slots),
        "transmission",
        (phase, params),
        floats(slots, WIN, 2 * WIN),
    )

    sends = call(
        functools.partial(column_kernel, (col_tiles, radix, row_tiles, slots, tile_rows)),
        "column_transform",
        (*arrived, jnp.asarray(column_tables(grid_len)), params),
        [floats(slots, WIN, 2 * WIN)] * row_tiles,
        scratch=(
            pltpu.VMEM((radix, WIN, 4 * WIN), f32),
            pltpu.VMEM((grid_len + WIN, 4 * WIN), f32),
        ),
        flops=24 * grid_len * WIN * 2 * WIN,
        moved=4 << 20,
    )
    parts = [sends[0]] + [shift(sends[k], "beam", k) for k in range(1, row_tiles)]

    return call(
        functools.partial(pattern_kernel, row_tiles, slots),
        "patterns",
        (*parts, transmit, *(jnp.asarray(table) for table in window_tables())),
        floats(1, 1, slots, WIN, WIN),
        flops=48 * slots * WIN * WIN * WIN,
        moved=2 << 20,
    )


def solution(mesh):
    return jax.shard_map(
        local,
        mesh=mesh,
        in_specs=(
            P(None, ("phonon", "beam"), "row", None),
            P(("phonon", "beam"), "row"),
            P(),
            P(),
            P(),
            P(),
            P(),
        ),
        out_specs=P(("phonon", "beam"), "row", None, None, None),
        check_vma=False,
    )
```

```python
import functools
import math

import jax
import jax.numpy as jnp
import numpy as np
from jax import lax
from jax.experimental import pallas as pl
from jax.experimental.pallas import tpu as pltpu
from jax.sharding import PartitionSpec as P

WIN = 128
CHUNKS = 2
HALF = WIN // CHUNKS
LANES = 2 * HALF

prop_coef = 3e-05
f32, bf16 = jnp.float32, jnp.bfloat16


def shift(shard, axis, by):
    devices = lax.axis_size(axis)
    return lax.ppermute(shard, axis, [(i, (i + by) % devices) for i in range(devices)])


def split_table(table):
    high = np.asarray(table, np.float32).astype(bf16)
    low = (np.asarray(table, np.float64) - high.astype(np.float64)).astype(np.float32).astype(bf16)
    return high, low


def wave_table(length):
    index = np.arange(length)
    freq = np.where(index < length // 2, index, index - length).astype(np.float64)
    turns = (index[:, None] * index[None, :]) % length
    angle = 2.0 * math.pi / length * turns - prop_coef * (freq * freq)[:, None]
    return np.cos(angle) / math.sqrt(length), np.sin(angle) / math.sqrt(length)


def row_tables(length, tile_cols, tiles):
    real, imag = wave_table(length)
    cols = (np.arange(tiles)[:, None] * tile_cols + np.arange(WIN)[None, :]) % length
    cols = cols.reshape(tiles, CHUNKS, HALF)
    both = np.concatenate([real[:, cols], imag[:, cols]], axis=3)
    return split_table(np.transpose(both, (2, 1, 0, 3)))


def column_tables(length):
    radix = length // WIN
    real, imag = wave_table(length)
    parts = []
    for k0 in range(radix):
        both = np.concatenate([real[k0::radix, :WIN].T, imag[k0::radix, :WIN].T], axis=0)
        high, low = split_table(both)
        parts.append(np.concatenate([high, low, high], axis=1))
    return np.stack(parts)


def window_tables():
    index = np.arange(WIN)
    angle = -2.0 * math.pi / WIN * ((index[:, None] * index[None, :]) % WIN)
    real, imag = np.cos(angle) / math.sqrt(WIN), np.sin(angle) / math.sqrt(WIN)
    left = np.concatenate([real, imag], axis=1)
    rows = []
    for chunk in range(CHUNKS):
        at = slice(chunk * HALF, (chunk + 1) * HALF)
        rows += [np.concatenate([real[at], imag[at]], 1), np.concatenate([-imag[at], real[at]], 1)]
    return split_table(left) + split_table(np.concatenate(rows, axis=0))


def split(value):
    high = value.astype(bf16)
    return high, (value - high.astype(f32)).astype(bf16)


def mul(left, right):
    return jnp.dot(left, right, preferred_element_type=f32)


def signs(rows):
    lane = lax.broadcasted_iota(jnp.int32, (rows, LANES), 1)
    return jnp.where(lane < HALF, -1.0, 1.0).astype(f32)


def swap(value):
    return pltpu.roll(value, HALF, 1)


def row_kernel(tiles, step, spectra, high, low, *messages):
    me = lax.axis_index("row")
    rows = spectra.shape[2]
    sign = signs(rows)
    lhs_high, lhs_low = split(jnp.concatenate([spectra[0, 0], spectra[1, 0]], axis=0))
    for k in range(0, tiles, 2):
        pair = [lax.rem(me + k + n, tiles) for n in range(2)]
        table = jnp.concatenate([high[0, tile] for tile in pair], axis=1)
        small = jnp.concatenate([low[0, tile] for tile in pair], axis=1)
        both = mul(lhs_high, table) + mul(lhs_low, table) + mul(lhs_high, small)
        for n in range(2):
            piece = both[:, n * LANES : (n + 1) * LANES]
            wave = piece[:rows] + sign * swap(piece[rows:])
            for block, to in enumerate((k + n, (k + n - step) % tiles)):
                messages[to][block] = wave


def prep_kernel(sizes, slots_ref, corners, freq, amp_re, amp_im, cosine, sine, params):
    row_tiles, col_tiles, slots, probes, tile_rows, tile_cols, grid_len = sizes
    beam_pos, row_pos = lax.axis_index("beam"), lax.axis_index("row")
    for k in range(row_tiles):
        tile = target(k, beam_pos, row_tiles)
        for s in range(slots):
            probe = slots_ref[(tile * col_tiles + row_pos) * slots + s]
            live = (probe < probes).astype(f32)
            safe = jnp.minimum(probe, probes - 1)
            top, left = corners[2 * safe], corners[2 * safe + 1]
            turns = lax.rem(top * freq[2 * beam_pos] + left * freq[2 * beam_pos + 1], grid_len)
            turns = lax.rem(turns + grid_len, grid_len)
            re, im = amp_re[beam_pos] * live, amp_im[beam_pos] * live
            c, n = cosine[turns], sine[turns]
            values = [
                re * c - im * n,
                re * n + im * c,
                jnp.clip(top - tile * tile_rows, 0, tile_rows - 1).astype(f32),
                jnp.clip(left - row_pos * tile_cols, 0, tile_cols - 1).astype(f32),
            ]
            for at, value in enumerate(values):
                params[k * slots + s, at] = jnp.full((LANES,), value, f32)


def masks_of(params, at, chunk):
    row = lax.broadcasted_iota(jnp.int32, (WIN, LANES), 0).astype(f32)
    lane = lax.broadcasted_iota(jnp.int32, (WIN, LANES), 1)
    col = (jnp.where(lane < HALF, lane, lane - HALF) + chunk * HALF).astype(f32)
    return row >= params[at, 2:3, :], col >= params[at, 3:4, :]


def pick(rows_here, cols_here, near_near, near_far, far_near, far_far):
    return jnp.where(
        rows_here,
        jnp.where(cols_here, near_near, near_far),
        jnp.where(cols_here, far_near, far_far),
    )


def transmit_kernel(slots, phase, params, out):
    sign = signs(WIN)
    for chunk in range(CHUNKS):
        at = slice(chunk * HALF, (chunk + 1) * HALF)
        after = slice(WIN + chunk * HALF, WIN + (chunk + 1) * HALF)
        blocks = [
            jnp.concatenate([phase[rows, cols]] * 2, axis=1)
            for rows in (slice(0, WIN), slice(WIN, 2 * WIN))
            for cols in (at, after)
        ]
        for s in range(slots):
            value = pick(*masks_of(params, s, chunk), *blocks)
            out[chunk, s, 0] = jnp.cos(value)
            out[chunk, s, 1] = jnp.sin(value) * sign


def column_kernel(sizes, chunk, *refs):
    sources, radix, row_tiles, slots, tile_rows = sizes
    arrived, (table, params) = refs[:sources], refs[sources : sources + 2]
    sends = refs[sources + 2 : sources + 2 + row_tiles]
    gathered, waves = refs[sources + 2 + row_tiles :]
    row_pos, beam_pos = lax.axis_index("row"), lax.axis_index("beam")
    part = arrived[0].shape[1] // radix
    grid_len = radix * WIN
    sign = signs(WIN)
    for k in range(sources):
        source = lax.rem(row_pos + sources - k, sources)
        at = pl.ds(pl.multiple_of(source * part, part), part)
        for k0 in range(radix):
            for block in range(2):
                gathered[k0, at, block * LANES : (block + 1) * LANES] = arrived[k][
                    block, pl.ds(k0, part, stride=radix), :
                ]
    pieces = []
    for k0 in range(radix):
        high, low = split(gathered[k0])
        both = mul(table[k0], jnp.concatenate([high, high, low], axis=0))
        halves = []
        for block in range(2):
            piece = both[:, block * LANES : (block + 1) * LANES]
            halves.append(piece[:WIN] + sign * swap(piece[WIN:]))
        pieces.append(halves)
    for block in range(2):
        at = slice(block * LANES, (block + 1) * LANES)
        zero, one, two, three = (pieces[k0][block] for k0 in range(radix))
        even, odd = zero + two, one + three
        even_turned, odd_turned = zero - two, sign * swap(one - three)
        rows = [even + odd, even_turned + odd_turned, even - odd, even_turned - odd_turned]
        for a in range(radix + 1):
            waves[a * WIN : (a + 1) * WIN, at] = rows[a % radix]
    for k in range(row_tiles):
        start = target(k, beam_pos, row_tiles) * tile_rows
        near = pl.ds(pl.multiple_of(start, 8), WIN)
        far = pl.ds(pl.multiple_of(lax.rem(start + WIN, grid_len), 8), WIN)
        for s in range(slots):
            which = k * slots + s
            first, second = slice(0, LANES), slice(LANES, 2 * LANES)
            wave = pick(
                *masks_of(params, which, chunk),
                waves[near, first],
                waves[near, second],
                waves[far, first],
                waves[far, second],
            )
            coef_re, coef_im = params[which, 0:1, :], params[which, 1:2, :]
            sends[k][s] = wave * coef_re + (sign * coef_im) * swap(wave)


def pattern_kernel(slots, *refs):
    transmit, left_high, left_low, right_high, right_low, out = refs[-6:]
    arrived = refs[:-6]
    each = len(arrived) // CHUNKS
    sign = signs(WIN)
    values, turned = [], []
    for s in range(slots):
        for chunk in range(CHUNKS):
            wave = arrived[chunk * each][s]
            for part in arrived[chunk * each + 1 : (chunk + 1) * each]:
                wave = wave + part[s]
            wave = wave * transmit[chunk, s, 0] + swap(wave) * transmit[chunk, s, 1]
            values.append(wave)
            turned.append(sign * swap(wave))
    window = jnp.concatenate(
        [jnp.concatenate(values, axis=1), jnp.concatenate(turned, axis=1)], axis=0
    )
    high, low = split(window)
    inner = mul(left_high[...], high) + mul(left_high[...], low) + mul(left_low[...], high)
    inner = jnp.concatenate(
        [inner[:, s * 2 * WIN : (s + 1) * 2 * WIN] for s in range(slots)], axis=0
    )
    high, low = split(inner)
    outer = mul(high, right_high[...]) + mul(low, right_high[...]) + mul(high, right_low[...])
    power = outer[:, :WIN] * outer[:, :WIN] + outer[:, WIN:] * outer[:, WIN:]
    for s in range(slots):
        out[0, 0, s] = power[s * WIN : (s + 1) * WIN]


def on_line(devices):
    return devices == 4


def target(k, beam_pos, devices):
    if not on_line(devices):
        return lax.rem(beam_pos + k, devices)
    first = jnp.where(beam_pos % 2 == 0, 3, 0)
    second = jnp.where(beam_pos < 2, 2, 1)
    return [beam_pos, first, second, 6 - beam_pos - first - second][k]


def sum_over_beams(sends):
    devices = len(sends)
    if not on_line(devices):
        return [sends[0]] + [shift(sends[k], "beam", k) for k in range(1, devices)]
    own, first, second, third = sends
    beam_pos = lax.axis_index("beam")
    inside = (beam_pos == 1) | (beam_pos == 2)
    one = lax.ppermute(first, "beam", [(0, 1), (1, 0), (2, 3), (3, 2)])
    two = lax.ppermute(second, "beam", [(1, 2), (2, 1)])
    three = lax.ppermute(second, "beam", [(0, 2), (3, 1)])
    relayed = jnp.where(inside, third + one, third)
    four = lax.ppermute(relayed, "beam", [(0, 1), (1, 3), (2, 0), (3, 2)])
    return [own + jnp.where(inside, two, one), three, four]


def call(kernel, name, ins, outs, smem=(), scratch=(), flops=0, moved=0):
    vmem, scalar = pl.BlockSpec(memory_space=pltpu.VMEM), pl.BlockSpec(memory_space=pltpu.SMEM)
    return pl.pallas_call(
        kernel,
        name=name,
        out_shape=outs,
        in_specs=[scalar if at in smem else vmem for at in range(len(ins))],
        out_specs=jax.tree.map(lambda _: vmem, outs),
        scratch_shapes=list(scratch),
        cost_estimate=pl.CostEstimate(flops=flops, bytes_accessed=moved, transcendentals=0),
    )(*ins)


def local(spectra, potential, amp_re, amp_im, beam_freq, probe_corners, slot_table):
    ky_rows, grid_len = spectra.shape[2], spectra.shape[3]
    tile_rows, tile_cols = potential.shape
    row_tiles, col_tiles, slots = slot_table.shape
    probes = probe_corners.shape[0]
    radix = grid_len // WIN

    def floats(*shape):
        return jax.ShapeDtypeStruct(shape, f32)

    row_high, row_low = row_tables(grid_len, tile_cols, col_tiles)
    arrived = []
    for chunk in range(CHUNKS):
        messages = call(
            functools.partial(row_kernel, col_tiles, WIN // tile_cols),
            f"row_transform_{chunk}",
            (
                spectra,
                jnp.asarray(row_high[chunk : chunk + 1]),
                jnp.asarray(row_low[chunk : chunk + 1]),
            ),
            [floats(2, ky_rows, LANES)] * col_tiles,
            flops=24 * ky_rows * grid_len * HALF * col_tiles,
            moved=4 << 20,
        )
        order = sorted(range(1, col_tiles), key=lambda k: -min(k, col_tiles - k))
        moved = {k: shift(messages[k], "row", k) for k in order}
        arrived.append([messages[0]] + [moved[k] for k in range(1, col_tiles)])

    index = np.arange(grid_len)
    angle = -2.0 * math.pi / grid_len * index
    params = call(
        functools.partial(
            prep_kernel,
            (row_tiles, col_tiles, slots, probes, tile_rows, tile_cols, grid_len),
        ),
        "slot_parameters",
        (
            slot_table.reshape(-1),
            probe_corners.reshape(-1),
            beam_freq.reshape(-1),
            amp_re,
            amp_im,
            jnp.asarray(np.cos(angle), f32),
            jnp.asarray(np.sin(angle), f32),
        ),
        floats(row_tiles * slots, 8, LANES),
        smem=range(7),
    )

    below = [potential] + [shift(potential, "beam", -k) for k in range(1, WIN // tile_rows + 1)]
    tall = jnp.concatenate(below, axis=0)
    beside = [tall] + [shift(tall, "row", -k) for k in range(1, WIN // tile_cols + 1)]
    phase = jnp.concatenate(beside, axis=1)
    phase = jnp.pad(phase, [(0, 2 * WIN - length) for length in phase.shape])
    transmit = call(
        functools.partial(transmit_kernel, slots),
        "transmission",
        (phase, params),
        floats(CHUNKS, slots, 2, WIN, LANES),
    )

    table = jnp.asarray(column_tables(grid_len))
    parts = []
    for chunk in range(CHUNKS):
        sends = call(
            functools.partial(
                column_kernel, (col_tiles, radix, row_tiles, slots, tile_rows), chunk
            ),
            f"column_transform_{chunk}",
            (*arrived[chunk], table, params),
            [floats(slots, WIN, LANES)] * row_tiles,
            scratch=(
                pltpu.VMEM((radix, WIN, 2 * LANES), f32),
                pltpu.VMEM((grid_len + WIN, 2 * LANES), f32),
            ),
            flops=24 * grid_len * WIN * 2 * HALF,
            moved=2 << 20,
        )
        parts += sum_over_beams(sends)

    return call(
        functools.partial(pattern_kernel, slots),
        "patterns",
        (*parts, transmit, *(jnp.asarray(table) for table in window_tables())),
        floats(1, 1, slots, WIN, WIN),
        flops=48 * slots * WIN * WIN * WIN,
        moved=2 << 20,
    )


def solution(mesh):
    return jax.shard_map(
        local,
        mesh=mesh,
        in_specs=(
            P(None, ("phonon", "beam"), "row", None),
            P(("phonon", "beam"), "row"),
            P(),
            P(),
            P(),
            P(),
            P(),
        ),
        out_specs=P(("phonon", "beam"), "row", None, None, None),
        check_vma=False,
    )
```
